32 devices in a mesh: dp: 4 (over y, core), mp: 8 (over z, x).
Axes of the slice: x: 2, y: 2, z: 4, core: 2. Of those that a mesh axis runs over, the one named last changes fastest.
Arguments:
- block_in: bfloat16 [8192, 768], P(('dp', 'mp')), may hold values from -6 to 6
- segment_ids: int32 [8192], P('dp'), may hold values from 0 to 8191, as said below
- w_qkv: bfloat16 [768, 2304], P(('dp', 'mp')), may hold values from -0.21875 to 0.21875
- w_out: bfloat16 [768, 768], P(('dp', 'mp')), may hold values from -0.875 to 0.875
- conv_taps: bfloat16 [768, 3, 3], P(('dp', 'mp')), may hold values from -4 to 4
- norm_gain: bfloat16 [768, 2], P(('dp', 'mp')), may hold values from 0.5 to 1.5
- norm_bias: bfloat16 [768, 2], P(('dp', 'mp')), may hold values from -3 to 3
- w_up: bfloat16 [768, 3072], P(None, 'mp'), may hold values from -0.21875 to 0.21875
- w_down: bfloat16 [3072, 768], P('mp'), may hold values from -0.109375 to 0.109375
- out_grad: bfloat16 [8192, 768], P(('dp', 'mp')), may hold values from -6 to 6
Outputs:
- block_out: bfloat16 [8192, 768], P(('dp', 'mp'))
- input_grad: float32 [8192, 768], P(('dp', 'mp'))
- qkv_grad: float32 [768, 2304], P(('dp', 'mp'))
- proj_grad: float32 [768, 768], P(('dp', 'mp'))
- conv_grad: float32 [768, 3, 3], P(('dp', 'mp'))
- gain_grad: float32 [768, 2], P(('dp', 'mp'))
- bias_grad: float32 [768, 2], P(('dp', 'mp'))
- up_grad: float32 [768, 3072], P(None, 'mp')
- down_grad: float32 [3072, 768], P('mp')
The draws below stay inside these ranges and needn't reach their ends.
Inputs may be any that keep to these rules, and one draw needn't show every extreme that they name: `segment_ids`: segment ids never fall along the tokens, and tokens with equal ids form one document. A token's id is its packed sequence times 2048 plus the place, within that sequence, of its document's last token. The first token of each packed sequence is a document of its own; each document holds at most 1024 tokens, and every packed sequence has one of exactly that many.
All inputs are finite; a program needn't handle non-finite values.
Results may differ from the reference program's by a relative error of at most 0.018.
The reference program's roundings to bfloat16 on the way count: a program that leaves them out, or rounds other values in their place, can miss the bound.
Values may be sent and summed in bfloat16 or wider, within the bound.
A program may use at most 128 MiB of HBM per device.

```python
import jax
import jax.numpy as jnp
from jax import lax

D = 768
HEADS = 12
HEAD_DIM = 64
FF = 3072
TOK_DEV = 256
SEQ_LEN = 2048
QB = 256
TOKENS = 8192


def draw_segment_ids(key, part):
    count_seq = TOKENS // SEQ_LEN
    blocks = SEQ_LEN // TOK_DEV
    half_blocks = blocks // 2
    key_a, key_b, key_c, key_d = jax.random.split(jax.random.fold_in(key, 11), 4)
    first = jax.random.randint(key_a, (count_seq,), 0, half_blocks)
    inside = jax.random.randint(key_b, (count_seq,), 2, TOK_DEV)
    long_start = first * TOK_DEV + inside
    long_end = long_start + SEQ_LEN // 2
    offsets = jax.random.randint(key_c, (count_seq, blocks), 2, TOK_DEV)
    taken = jax.random.randint(key_d, (count_seq, blocks), 0, 2)
    candidate = jnp.arange(blocks, dtype=jnp.int32)[None, :] * TOK_DEV + offsets
    valid = (taken == 1) & ((candidate < long_start[:, None]) | (candidate > long_end[:, None]))
    places = jnp.arange(SEQ_LEN, dtype=jnp.int32)
    marked = jnp.any((candidate[:, :, None] == places[None, None, :]) & valid[:, :, None], axis=1)
    starts = marked | (places[None, :] <= 1) | (places[None, :] == long_start[:, None]) | (places[None, :] == long_end[:, None])
    next_start = jnp.concatenate([starts[:, 1:], jnp.ones((count_seq, 1), dtype=bool)], axis=1)
    end_mark = jnp.where(next_start, places[None, :], SEQ_LEN).astype(jnp.int32)
    ends = lax.cummin(end_mark, axis=1, reverse=True)
    base = jnp.arange(count_seq, dtype=jnp.int32)[:, None] * SEQ_LEN
    return (base + ends).reshape(-1).astype(jnp.int32)


def shard_levels(stream_key, extent, cuts, least, high):
    def one(position, blocks):
        heights = jax.random.uniform(jax.random.fold_in(jax.random.fold_in(stream_key, 6), position), (blocks,), jnp.float32, least / len(cuts), high / len(cuts))
        return jnp.repeat(jnp.exp(heights), extent[position] // blocks).reshape((-1,) + (1,) * (len(extent) - position - 1))

    loudness = one(*cuts[0])
    for cut in cuts[1:]:
        loudness = loudness * one(*cut)
    return loudness


def noise(own_key, extent, deviation, bound, pieces=(), kind=jnp.bfloat16):
    factor_of = shard_levels(own_key, extent, pieces, -0.22, 0.18) if pieces else 1.0
    drawn = jax.random.normal(own_key, extent, jnp.float32) * deviation * factor_of
    return jnp.minimum(jnp.maximum(drawn, -bound), bound).astype(kind)


def setup_inputs(seed: int = 0) -> dict:
    arg_keys = jax.random.split(jax.random.key(seed), 11)
    return {
        "block_in": noise(arg_keys[0], (TOKENS, D), 1.0, 6.0, ((0, 32),)),
        "segment_ids": draw_segment_ids(jax.random.fold_in(arg_keys[10], 71), 0),
        "w_qkv": noise(arg_keys[2], (D, 3 * D), D ** -0.5, 0.21875, ((0, 32),)),
        "w_out": noise(arg_keys[3], (D, D), (D // 16) ** -0.5, 0.875, ((0, 32),)),
        "conv_taps": noise(arg_keys[4], (D, 3, 3), 0.8, 4.0, ((0, 32),)),
        "norm_gain": jnp.clip(1.0 + 0.1 * jax.random.normal(arg_keys[5], (D, 2), jnp.float32), 0.5, 1.5).astype(jnp.bfloat16),
        "norm_bias": noise(arg_keys[6], (D, 2), 0.5, 3.0, ((0, 32),)),
        "w_up": noise(arg_keys[7], (D, FF), D ** -0.5, 0.21875, ((1, 8),)),
        "w_down": noise(arg_keys[8], (FF, D), FF ** -0.5, 0.109375, ((0, 8),)),
        "out_grad": noise(arg_keys[9], (TOKENS, D), 1.0, 6.0, ((0, 32),)),
    }


precise = lax.Precision.HIGHEST
eps_norm = 1e-05

@jax.custom_vjp
def low(v):
    return lax.optimization_barrier(v.astype(jnp.bfloat16)).astype(jnp.float32)

@jax.custom_vjp
def low_back(v):
    return v

def low_keep(v):
    return (low(v), None)

def low_pass(kept, grad):
    return (grad,)

def back_keep(v):
    return (v, None)

def back_low(kept, grad):
    return (low(grad),)
low.defvjp(low_keep, low_pass)
low_back.defvjp(back_keep, back_low)

def layer_norm(rows, gain, bias):
    average = lax.optimization_barrier(jnp.mean(rows, axis=-1, keepdims=True))
    centered = rows - average
    spread = lax.optimization_barrier(jnp.mean(centered * centered, axis=-1, keepdims=True))
    return centered * lax.rsqrt(spread + eps_norm) * gain + bias

def depth_conv(pre, taps, segs):
    length = pre.shape[0]
    total = pre * taps[0]
    for lag in (1, 2):
        source = jnp.concatenate([jnp.zeros((lag, pre.shape[1]), jnp.float32), pre[:length - lag]], axis=0)
        there = jnp.concatenate([jnp.full((lag,), -1, jnp.int32), segs[:length - lag]])
        keep = (there == segs)[:, None]
        total = total + jnp.where(keep, source, 0.0) * taps[lag]
    return total

def sequence_block(rows, segs, params):
    w_qkv, w_out, conv_taps, norm_gain, norm_bias, w_up, w_down = params
    length = rows.shape[0]
    taps = conv_taps.transpose(1, 0, 2).reshape(3 * D, 3).T
    normed1 = low(layer_norm(rows, norm_gain[:, 0], norm_bias[:, 0]))
    pre = low_back(jnp.dot(normed1, w_qkv, precision=precise))
    mixed_qkv = low(depth_conv(pre, taps, segs))
    queries = mixed_qkv[:, :D].reshape(length, HEADS, HEAD_DIM)
    keys = mixed_qkv[:, D:2 * D].reshape(length, HEADS, HEAD_DIM)
    values = mixed_qkv[:, 2 * D:].reshape(length, HEADS, HEAD_DIM)
    places = jnp.arange(length, dtype=jnp.int32)
    blocks = length // QB

    def attend(piece):
        block_q, q_places, q_segs = piece
        scores = jnp.einsum('qhd,khd->hqk', block_q, keys, precision=precise) * HEAD_DIM ** (-0.5)
        allowed = (places[None, :] <= q_places[:, None]) & (segs[None, :] == q_segs[:, None])
        scores = low_back(jnp.where(allowed[None], scores, -1e+30))
        shifted = jnp.exp(scores - lax.optimization_barrier(jnp.max(scores, axis=-1, keepdims=True)))
        probs = low(shifted / lax.optimization_barrier(jnp.sum(shifted, axis=-1, keepdims=True)))
        return jnp.einsum('hqk,khd->qhd', probs, values, precision=precise).reshape(QB, D)
    attended = lax.map(jax.checkpoint(attend), (queries.reshape(blocks, QB, HEADS, HEAD_DIM), places.reshape(blocks, QB), segs.reshape(blocks, QB)))
    attended = low_back(low(attended.reshape(length, D)))
    mixed = low_back(jnp.dot(attended, w_out, precision=precise))
    residual = rows + mixed
    normed2 = low(layer_norm(residual, norm_gain[:, 1], norm_bias[:, 1]))
    upper = low_back(jnp.dot(normed2, w_up, precision=precise))
    hidden = low(jnp.square(jnp.maximum(upper, 0.0)))
    return residual + low_back(jnp.dot(hidden, w_down, precision=precise))

def reference(block_in, segment_ids, w_qkv, w_out, conv_taps, norm_gain, norm_bias, w_up, w_down, out_grad):
    floats = (block_in.astype(jnp.float32), w_qkv.astype(jnp.float32), w_out.astype(jnp.float32), conv_taps.astype(jnp.float32), norm_gain.astype(jnp.float32), norm_bias.astype(jnp.float32), w_up.astype(jnp.float32), w_down.astype(jnp.float32))
    count = TOKENS // SEQ_LEN
    seg_rows = segment_ids.reshape(count, SEQ_LEN)

    def forward(inputs, p_qkv, p_out, p_taps, p_gain, p_bias, p_up, p_down):
        params = (p_qkv, p_out, p_taps, p_gain, p_bias, p_up, p_down)

        def single(pair):
            return sequence_block(pair[0], pair[1], params)
        outputs = lax.map(jax.checkpoint(single), (inputs.reshape(count, SEQ_LEN, D), seg_rows))
        return outputs.reshape(TOKENS, D)
    result, pull = jax.vjp(forward, *floats)
    grads = pull(out_grad.astype(jnp.float32))
    return (result.astype(jnp.bfloat16), grads[0], grads[1], grads[2], grads[3], grads[4], grads[5], grads[6], grads[7])
```

```python
import functools

import jax
import jax.numpy as jnp
from jax import lax
from jax.experimental import pallas as pl
from jax.experimental.pallas import tpu as pltpu
from jax.sharding import PartitionSpec as P

HEAD_DIM = 64


eps_norm = 1e-05


def from_behind(value, axis, steps):
    count = lax.axis_size(axis)
    leading, last = (max(0, -steps), min(count, count - steps))
    return lax.ppermute(value, axis, [(source, source + steps) for source in range(leading, last)])


def layer_norm(rows, gain, bias):
    average = jnp.mean(rows, axis=-1, keepdims=True)
    centered = rows - average
    spread = jnp.mean(centered * centered, axis=-1, keepdims=True)
    inverse = lax.rsqrt(spread + eps_norm)
    normal = centered * inverse
    return (normal * gain + bias, normal, inverse)


def norm_back(grad, normal, inverse, gain):
    scaled = grad * gain
    inner = (
        scaled
        - jnp.mean(scaled, axis=-1, keepdims=True)
        - normal * jnp.mean(scaled * normal, axis=-1, keepdims=True)
    )
    return (inner * inverse, jnp.sum(grad * normal, axis=0), jnp.sum(grad, axis=0))


def tap_keep(segs, places, here, there, count, seq_len):
    same_segment = segs[here : here + count] == segs[there : there + count]
    same_sequence = (
        places[here : here + count] // seq_len == places[there : there + count] // seq_len
    )
    return (same_segment & same_sequence)[:, None]


def conv_apply(pre_wide, taps, segs, places, seq_len):
    count = pre_wide.shape[0] - 2
    total = jnp.zeros((count, pre_wide.shape[1]), jnp.float32)
    for lag in range(3):
        keep = tap_keep(segs, places, 2, 2 - lag, count, seq_len)
        total = total + jnp.where(keep, pre_wide[2 - lag : 2 - lag + count], 0.0) * taps[lag]
    return total


def conv_back(grad_wide, taps, segs, places, seq_len):
    count = grad_wide.shape[0] - 2
    total = jnp.zeros((count, grad_wide.shape[1]), jnp.float32)
    for lag in range(3):
        keep = tap_keep(segs, places, lag, 0, count, seq_len)
        total = total + jnp.where(keep, grad_wide[lag : lag + count], 0.0) * taps[lag]
    return total


def taps_back(pre_wide, grad, segs, places, seq_len):
    count = grad.shape[0]
    results = []
    for lag in range(3):
        keep = tap_keep(segs, places, 2, 2 - lag, count, seq_len)
        results.append(
            jnp.sum(jnp.where(keep, pre_wide[2 - lag : 2 - lag + count] * grad, 0.0), axis=0)
        )
    return jnp.stack(results)


def contract_first(left, right):
    return lax.dot_general(
        left, right, (((0,), (0,)), ((), ())), preferred_element_type=jnp.float32
    )


def contract_last(left, right):
    return lax.dot_general(
        left, right, (((1,), (1,)), ((), ())), preferred_element_type=jnp.float32
    )


def on_device_rings(
    block_in, segment_ids, w_qkv, w_out, conv_taps, norm_gain, norm_bias, w_up, w_down, out_grad
):
    rows, width = block_in.shape
    heads = width // HEAD_DIM
    block = min(512, rows)
    reach = lax.axis_size("mp")
    seq_len = rows * reach
    scale = HEAD_DIM ** (-0.5)
    model_index = lax.axis_index("mp")
    start = model_index * rows
    offset = (reach - 1 - model_index) * rows
    seq_begin = start - model_index * rows
    full_qkv, full_out, full_taps, full_gain, full_bias = (
        lax.all_gather(w_qkv, ("dp", "mp"), axis=0, tiled=True),
        lax.all_gather(w_out, ("dp", "mp"), axis=0, tiled=True),
        lax.all_gather(conv_taps, ("dp", "mp"), axis=0, tiled=True),
        lax.all_gather(norm_gain, ("dp", "mp"), axis=0, tiled=True),
        lax.all_gather(norm_bias, ("dp", "mp"), axis=0, tiled=True),
    )
    gains = full_gain.astype(jnp.float32)
    biases = full_bias.astype(jnp.float32)
    taps = full_taps.astype(jnp.float32).transpose(1, 0, 2).reshape(3 * width, 3).T
    padding = jnp.full((2,), -1, jnp.int32)
    padded_segs = jnp.concatenate([padding, segment_ids, padding])
    back_segs = lax.dynamic_slice_in_dim(padded_segs, start, rows + 2)
    back_places = start - 2 + jnp.arange(rows + 2, dtype=jnp.int32)
    ahead_segs = lax.dynamic_slice_in_dim(padded_segs, start + 2, rows + 2)
    ahead_places = start + jnp.arange(rows + 2, dtype=jnp.int32)
    inputs = block_in.astype(jnp.float32)
    normed1_full, normal1, inverse1 = layer_norm(inputs, gains[:, 0], biases[:, 0])
    normed1 = normed1_full.astype(jnp.bfloat16)
    pre_own = jnp.dot(normed1, full_qkv, preferred_element_type=jnp.float32)
    rim = from_behind(pre_own[rows - 2 :], "mp", 1)
    pre_wide = jnp.concatenate([rim, pre_own], axis=0)
    mixed_qkv = conv_apply(pre_wide, taps, back_segs, back_places, seq_len).astype(jnp.bfloat16)
    query_rows = mixed_qkv[:, :width]
    pair_own = mixed_qkv[:, width:]
    window_start = jnp.zeros((reach * rows, 2 * width), jnp.bfloat16)
    window_start = lax.dynamic_update_slice_in_dim(window_start, pair_own, (reach - 1) * rows, 0)

    def pass_step(distance, carry):
        piece, gathered = carry
        piece = from_behind(piece, "mp", 1)
        gathered = lax.dynamic_update_slice_in_dim(
            gathered, piece, (reach - 1 - distance) * rows, 0
        )
        return (piece, gathered)

    unused_piece, window = lax.fori_loop(1, reach, pass_step, (pair_own, window_start))

    def fetch(queries, query_places, query_segs, index):
        pair = lax.dynamic_slice_in_dim(window, offset + index * block, block, 0)
        keys = pair[:, :width].reshape(block, heads, HEAD_DIM)
        values = pair[:, width:].reshape(block, heads, HEAD_DIM)
        key_places = seq_begin + index * block + jnp.arange(block, dtype=jnp.int32)
        key_segs = lax.dynamic_slice_in_dim(segment_ids, seq_begin + index * block, block)
        allowed = (
            (key_places[None, :] <= query_places[:, None])
            & (key_segs[None, :] == query_segs[:, None])
        )[None]
        scores = (
            jnp.einsum("qhd,khd->hqk", queries, keys, preferred_element_type=jnp.float32) * scale
        )
        return (keys, values, allowed, jnp.where(allowed, scores, -1e30))

    def block_setup(number):
        query_places = start + number * block + jnp.arange(block, dtype=jnp.int32)
        query_segs = lax.dynamic_slice_in_dim(segment_ids, start + number * block, block)
        queries = query_rows.reshape(block, heads, HEAD_DIM)
        count = (model_index * rows + number * block) // block + 1
        return (query_places, query_segs, queries, count)

    number = 0
    query_places, query_segs, queries, count = block_setup(number)

    def stats_step(index, carry):
        highest, total = carry
        keys, values, allowed, scores = fetch(queries, query_places, query_segs, index)
        new_high = jnp.maximum(highest, jnp.max(scores, axis=-1))
        total = total * jnp.exp(highest - new_high) + jnp.sum(
            jnp.where(allowed, jnp.exp(scores - new_high[..., None]), 0.0), axis=-1
        )
        return (new_high, total)

    highest, total = lax.fori_loop(
        0,
        count,
        stats_step,
        (jnp.full((heads, block), -1e30, jnp.float32), jnp.zeros((heads, block), jnp.float32)),
    )
    log_total = highest + jnp.log(total)

    def value_step(index, weighted):
        keys, values, allowed, scores = fetch(queries, query_places, query_segs, index)
        probs = jnp.where(allowed, jnp.exp(scores - log_total[..., None]), 0.0).astype(jnp.bfloat16)
        return weighted + jnp.einsum(
            "hqk,khd->qhd", probs, values, preferred_element_type=jnp.float32
        )

    weighted = lax.fori_loop(0, count, value_step, jnp.zeros((block, heads, HEAD_DIM), jnp.float32))
    attended_parts = weighted.reshape(block, width)
    log_parts = [log_total]
    attended = attended_parts.astype(jnp.bfloat16)
    mixed = jnp.dot(attended, full_out, preferred_element_type=jnp.float32)
    residual = inputs + mixed
    normed2_full, normal2, inverse2 = layer_norm(residual, gains[:, 1], biases[:, 1])
    normed2 = normed2_full.astype(jnp.bfloat16)
    normed2_rows = lax.all_gather(normed2, "mp", axis=0, tiled=True)
    upper = jnp.dot(normed2_rows, w_up, preferred_element_type=jnp.float32)
    hidden = jnp.square(jnp.maximum(upper, 0.0)).astype(jnp.bfloat16)
    ff_out = lax.psum_scatter(
        jnp.dot(hidden, w_down, preferred_element_type=jnp.float32).astype(jnp.bfloat16),
        "mp",
        scatter_dimension=0,
        tiled=True,
    ).astype(jnp.float32)
    block_out = (residual + ff_out).astype(jnp.bfloat16)
    grad_all = lax.all_gather(out_grad, "mp", axis=0, tiled=True)
    hidden_grad = contract_last(grad_all, w_down)
    upper_grad = (2.0 * jnp.maximum(upper, 0.0) * hidden_grad).astype(jnp.bfloat16)
    down_local = contract_first(hidden, grad_all)
    up_local = contract_first(normed2_rows, upper_grad)
    normed2_grad = lax.psum_scatter(
        contract_last(upper_grad, w_up).astype(jnp.bfloat16), "mp", scatter_dimension=0, tiled=True
    ).astype(jnp.float32)
    up_grad, down_grad = (
        lax.psum(up_local.astype(jnp.bfloat16), "dp").astype(jnp.float32),
        lax.psum(down_local.astype(jnp.bfloat16), "dp").astype(jnp.float32),
    )
    back2, gain2_grad, bias2_grad = norm_back(normed2_grad, normal2, inverse2, gains[:, 1])
    residual_grad = out_grad.astype(jnp.float32) + back2
    mixed_grad = residual_grad.astype(jnp.bfloat16)
    proj_local = contract_first(attended, mixed_grad)
    attended_grad = contract_last(mixed_grad, full_out).astype(jnp.bfloat16)
    window_grad = jnp.zeros((window.shape[0], 2 * width), jnp.float32)
    number = 0
    query_places, query_segs, queries, count = block_setup(number)
    log_total = log_parts[number]
    upstream = attended_grad.reshape(block, heads, HEAD_DIM)

    def delta_step(index, delta):
        keys, values, allowed, scores = fetch(queries, query_places, query_segs, index)
        probs = jnp.where(allowed, jnp.exp(scores - log_total[..., None]), 0.0)
        prob_grad = jnp.einsum("qhd,khd->hqk", upstream, values, preferred_element_type=jnp.float32)
        return delta + jnp.sum(probs * prob_grad, axis=-1)

    delta = lax.fori_loop(0, count, delta_step, jnp.zeros((heads, block), jnp.float32))

    def grad_step(index, carry):
        query_grad, window_grad = carry
        keys, values, allowed, scores = fetch(queries, query_places, query_segs, index)
        probs = jnp.where(allowed, jnp.exp(scores - log_total[..., None]), 0.0)
        prob_grad = jnp.einsum("qhd,khd->hqk", upstream, values, preferred_element_type=jnp.float32)
        score_grad = (probs * (prob_grad - delta[..., None])).astype(jnp.bfloat16)
        query_grad = (
            query_grad
            + jnp.einsum("hqk,khd->qhd", score_grad, keys, preferred_element_type=jnp.float32)
            * scale
        )
        key_grad = (
            jnp.einsum("hqk,qhd->khd", score_grad, queries, preferred_element_type=jnp.float32)
            * scale
        )
        value_grad = jnp.einsum(
            "hqk,qhd->khd", probs.astype(jnp.bfloat16), upstream, preferred_element_type=jnp.float32
        )
        update = jnp.concatenate(
            [key_grad.reshape(block, width), value_grad.reshape(block, width)], axis=1
        )
        place = offset + index * block
        current = lax.dynamic_slice_in_dim(window_grad, place, block, 0)
        window_grad = lax.dynamic_update_slice_in_dim(window_grad, current + update, place, 0)
        return (query_grad, window_grad)

    query_grad, window_grad = lax.fori_loop(
        0, count, grad_step, (jnp.zeros((block, heads, HEAD_DIM), jnp.float32), window_grad)
    )
    query_grads = query_grad.reshape(block, width)

    def window_slot(distance):
        return lax.dynamic_slice_in_dim(window_grad, (reach - 1 - distance) * rows, rows, 0)

    def back_step(step, gathered):
        distance = reach - 1 - step
        return from_behind(gathered.astype(jnp.bfloat16), "mp", -1).astype(
            gathered.dtype
        ) + window_slot(distance - 1)

    pair_grad = lax.fori_loop(0, reach - 1, back_step, window_slot(reach - 1))
    mix_grad = jnp.concatenate([query_grads, pair_grad], axis=1)
    ahead = from_behind(mix_grad[:2], "mp", -1)
    pre_grad = conv_back(
        jnp.concatenate([mix_grad, ahead], axis=0), taps, ahead_segs, ahead_places, seq_len
    ).astype(jnp.bfloat16)
    taps_local = taps_back(pre_wide, mix_grad, back_segs, back_places, seq_len)
    conv_local = taps_local.reshape(3, 3, width).transpose(2, 1, 0)
    normed1_grad = contract_last(pre_grad, full_qkv)
    qkv_local = contract_first(normed1, pre_grad)
    back1, gain1_grad, bias1_grad = norm_back(normed1_grad, normal1, inverse1, gains[:, 0])
    input_grad = residual_grad + back1
    gain_local = jnp.stack([gain1_grad, gain2_grad], axis=1)
    bias_local = jnp.stack([bias1_grad, bias2_grad], axis=1)
    qkv_grad, proj_grad, conv_grad, gain_grad, bias_grad = (
        lax.psum_scatter(qkv_local, ("dp", "mp"), scatter_dimension=0, tiled=True),
        lax.psum_scatter(proj_local, ("dp", "mp"), scatter_dimension=0, tiled=True),
        lax.psum_scatter(conv_local, ("dp", "mp"), scatter_dimension=0, tiled=True),
        lax.psum_scatter(gain_local, ("dp", "mp"), scatter_dimension=0, tiled=True),
        lax.psum_scatter(bias_local, ("dp", "mp"), scatter_dimension=0, tiled=True),
    )
    return (
        block_out,
        input_grad,
        qkv_grad,
        proj_grad,
        conv_grad,
        gain_grad,
        bias_grad,
        up_grad,
        down_grad,
    )


MESH = pl.DeviceIdType.MESH
VMEM_LIMIT = 62 * 1024 * 1024


class Spot:
    def __init__(self):
        dp = lax.axis_index("dp")
        mp = lax.axis_index("mp")
        self.y, self.c, self.z, self.x = dp // 2, dp % 2, mp // 2, mp % 2

    def at(self, y=None, c=None, z=None, x=None):
        y = self.y if y is None else y
        c = self.c if c is None else c
        z = self.z if z is None else z
        x = self.x if x is None else x
        return (y * 2 + c, z * 2 + x)

    def turn(self, k):
        return lax.rem(self.z + k, 4)

    def partners(self):
        yield self.at(y=1 - self.y)
        yield self.at(c=1 - self.c)
        yield self.at(x=1 - self.x)
        for k in (1, 2, 3):
            yield self.at(z=self.turn(k))


def greet(spot, extra=()):
    barrier = pltpu.get_barrier_semaphore()
    count = 0
    for device in list(spot.partners()) + list(extra):
        pl.semaphore_signal(barrier, inc=1, device_id=device, device_id_type=MESH)
        count += 1
    pl.semaphore_wait(barrier, count)


def send(source, target, send_sem, recv_sem, device):
    pltpu.make_async_remote_copy(
        src_ref=source,
        dst_ref=target,
        send_sem=send_sem,
        recv_sem=recv_sem,
        device_id=device,
        device_id_type=MESH,
    ).start()


def take(ref, sem):
    pltpu.make_async_copy(ref, ref, sem).wait()


def gather_kernel(
    wq, wo, pr, wu, wd, xr, WQ, WO, PR, WU, WD, XW,
    loc, a_z, a_x, a_y, a_c, a_s, u_z, u_x, u_c, u_s, d_z, d_x, d_y, d_c, d_s, h_r, h_s,
):
    spot = Spot()
    y, c, z, x = spot.y, spot.c, spot.z, spot.x
    quarter = y * 2 + c
    half = wu.shape[0] // 2
    wide = wu.shape[1]
    small = wd.shape[0] // 4
    to_x, to_y, to_c = spot.at(x=1 - x), spot.at(y=1 - y), spot.at(c=1 - c)
    arrays = ((wq, WQ), (wo, WO), (pr, PR))

    def up_piece(zz, xx):
        return WU.at[
            pl.ds(pl.multiple_of(c * half, half), half),
            pl.ds(pl.multiple_of((zz * 2 + xx) * wide, wide), wide),
        ]

    own_up = wu.at[pl.ds(pl.multiple_of(c * half, half), half), :]
    own_down = wd.at[pl.ds(pl.multiple_of(quarter * small, small), small), :]
    local = [
        pltpu.make_async_copy(own, full.at[y, c, z, x], loc.at[i])
        for i, (own, full) in enumerate(arrays)
    ]
    local.append(pltpu.make_async_copy(own_up, up_piece(z, x), loc.at[3]))
    local.append(pltpu.make_async_copy(own_down, WD.at[z, x, quarter], loc.at[4]))
    local.append(pltpu.make_async_copy(xr, XW.at[4], loc.at[5]))
    for copy in local:
        copy.start()
    greet(spot)

    for k in (1, 3, 2):
        for i, (own, full) in enumerate(arrays):
            send(own, full.at[y, c, z, x], a_s.at[i, 0], a_z.at[i, 3 - k], spot.at(z=spot.turn(k)))

    @pl.when(z < 3)
    def _():
        send(xr, XW.at[2], h_s.at[0], h_r.at[2], spot.at(z=z + 1))

    for i, (own, full) in enumerate(arrays):
        send(own, full.at[y, c, z, x], a_s.at[i, 1], a_x.at[i, 0], to_x)

    @pl.when(x == 0)
    def _():
        send(xr, XW.at[3], h_s.at[1], h_r.at[3], to_x)

    for i, (own, full) in enumerate(arrays):
        send(own, full.at[y, c, z, x], a_s.at[i, 2], a_y.at[i, 0], to_y)

    for k in (1, 3, 2):
        zz = spot.turn(k)
        for i, (own, full) in enumerate(arrays):
            piece = full.at[y, c, zz, x]
            take(piece, a_z.at[i, k - 1])
            send(piece, piece, a_s.at[i, 1], a_x.at[i, k], to_x)
            send(piece, piece, a_s.at[i, 2], a_y.at[i, 0], to_y)

    @pl.when(z >= 1)
    def _():
        take(XW.at[2], h_r.at[2])

        @pl.when(z < 3)
        def _():
            send(XW.at[2], XW.at[0], h_s.at[2], h_r.at[0], spot.at(z=z + 1))

        @pl.when(x == 0)
        def _():
            send(XW.at[2], XW.at[1], h_s.at[3], h_r.at[1], to_x)

        @pl.when(x == 1)
        def _():
            send(XW.at[2], XW.at[3], h_s.at[3], h_r.at[3], to_x)

    for k in (1, 3, 2):
        send(own_up, up_piece(z, x), u_s.at[0], u_z.at[3 - k], spot.at(z=spot.turn(k)))
    for k in (1, 3, 2):
        send(own_down, WD.at[z, x, quarter], d_s.at[0], d_z.at[3 - k], spot.at(z=spot.turn(k)))

    for k in range(4):
        zz = spot.turn(k)
        for i, (own, full) in enumerate(arrays):
            piece = full.at[y, c, zz, 1 - x]
            take(piece, a_x.at[i, k])
            send(piece, piece, a_s.at[i, 2], a_y.at[i, 1], to_y)

    @pl.when(z >= 2)
    def _():
        take(XW.at[0], h_r.at[0])

        @pl.when(x == 1)
        def _():
            send(XW.at[0], XW.at[1], h_s.at[4], h_r.at[1], to_x)

    for copy in local:
        copy.wait()
    for i, (own, full) in enumerate(arrays):
        send(full.at[y, c], full.at[y, c], a_s.at[i, 3], a_c.at[i], to_c)

    send(own_up, up_piece(z, x), u_s.at[1], u_x.at[0], to_x)
    send(own_down, WD.at[z, x, quarter], d_s.at[1], d_x.at[0], to_x)
    for i, (own, full) in enumerate(arrays):
        take(full.at[1 - y, c, :, x], a_y.at[i, 0])
        take(full.at[1 - y, c, :, 1 - x], a_y.at[i, 1])
        send(full.at[1 - y, c], full.at[1 - y, c], a_s.at[i, 3], a_c.at[i], to_c)
    send(own_down, WD.at[z, x, quarter], d_s.at[2], d_y, to_y)

    for k in (1, 3, 2):
        piece = up_piece(spot.turn(k), x)
        take(piece, u_z.at[k - 1])
        send(piece, piece, u_s.at[1], u_x.at[k], to_x)
    for k in (1, 3, 2):
        piece = WD.at[spot.turn(k), x, quarter]
        take(piece, d_z.at[k - 1])
        send(piece, piece, d_s.at[1], d_x.at[k], to_x)
        send(piece, piece, d_s.at[2], d_y, to_y)
    for k in range(4):
        take(up_piece(spot.turn(k), 1 - x), u_x.at[k])
    mine = WU.at[pl.ds(pl.multiple_of(c * half, half), half), :]
    other = WU.at[pl.ds(pl.multiple_of((1 - c) * half, half), half), :]
    send(mine, mine, u_s.at[2], u_c, to_c)
    for k in range(4):
        piece = WD.at[spot.turn(k), 1 - x, quarter]
        take(piece, d_x.at[k])
        send(piece, piece, d_s.at[2], d_y, to_y)
    send(WD.at[:, :, quarter], WD.at[:, :, quarter], d_s.at[3], d_c, to_c)
    across = (1 - y) * 2 + c
    take(WD.at[:, :, across], d_y)
    send(WD.at[:, :, across], WD.at[:, :, across], d_s.at[3], d_c, to_c)

    for i, (own, full) in enumerate(arrays):
        take(full.at[:, 1 - c], a_c.at[i])
    take(other, u_c)
    take(WD.at[:, :, pl.ds(0, 2)], d_c)

    @pl.when((x == 1) | (z >= 1))
    def _():
        take(XW.at[3], h_r.at[3])

    @pl.when(((x == 1) & (z >= 1)) | (z >= 2))
    def _():
        take(XW.at[1], h_r.at[1])

    for i, (own, full) in enumerate(arrays):
        take(full.at[0, 0, pl.ds(0, 3), 0], a_s.at[i, 0])
        take(full.at[0, 0, :, 0], a_s.at[i, 1])
        take(full.at[0, 0], a_s.at[i, 2])
        take(full.at[0], a_s.at[i, 3])
    take(WU.at[pl.ds(0, half), pl.ds(0, 3 * wide)], u_s.at[0])
    take(WU.at[pl.ds(0, half), pl.ds(0, 4 * wide)], u_s.at[1])
    take(mine, u_s.at[2])
    take(WD.at[pl.ds(0, 3), 0, 0], d_s.at[0])
    take(WD.at[:, 0, 0], d_s.at[1])
    take(WD.at[:, :, 0], d_s.at[2])
    take(WD.at[:, :, pl.ds(0, 2)], d_s.at[3])

    @pl.when(z < 3)
    def _():
        take(xr, h_s.at[0])

    @pl.when(x == 0)
    def _():
        take(xr, h_s.at[1])

    @pl.when(z >= 1)
    def _():
        @pl.when(z < 3)
        def _():
            take(xr, h_s.at[2])

        take(xr, h_s.at[3])

    @pl.when((z >= 2) & (x == 1))
    def _():
        take(xr, h_s.at[4])


def gather_all(w_qkv, w_out, small, w_up, w_down, rows):
    bf = jnp.bfloat16
    depth, width = w_qkv.shape[0], w_out.shape[1]
    dma = pltpu.SemaphoreType.DMA
    return pl.pallas_call(
        gather_kernel,
        out_shape=(
            jax.ShapeDtypeStruct((2, 2, 4, 2) + w_qkv.shape, bf),
            jax.ShapeDtypeStruct((2, 2, 4, 2) + w_out.shape, bf),
            jax.ShapeDtypeStruct((2, 2, 4, 2) + small.shape, jnp.float32),
            jax.ShapeDtypeStruct((w_up.shape[0], 8 * w_up.shape[1]), bf),
            jax.ShapeDtypeStruct((4, 2, 4, w_down.shape[0] // 4, width), bf),
            jax.ShapeDtypeStruct((5,) + rows.shape, bf),
        ),
        in_specs=[pl.BlockSpec(memory_space=pltpu.VMEM)] * 6,
        out_specs=[pl.BlockSpec(memory_space=pl.ANY)] * 6,
        scratch_shapes=[
            dma((6,)), dma((3, 3)), dma((3, 4)), dma((3, 2)), dma((3,)), dma((3, 4)),
            dma((3,)), dma((4,)), dma, dma((3,)),
            dma((3,)), dma((4,)), dma, dma, dma((4,)),
            dma((4,)), dma((5,)),
        ],
        compiler_params=pltpu.CompilerParams(
            collective_id=0, has_side_effects=True, vmem_limit_bytes=32 * 1024 * 1024
        ),
        name="gather_parameters",
    )(w_qkv, w_out, small, w_up, w_down, rows)


def add_pieces(count, body):
    lax.fori_loop(0, count, lambda i, carry: (body(i), carry)[1], 0)


def f32(value):
    return value.astype(jnp.float32)


def reduce_kernel(GQ, GO, SM, GU, GD, HN, OQ, OO, OS, OU, OD, OH, *scratch):
    (
        qc, qb, qy, qy2, qx, qx2, qz,
        oc, ob, oy, oy2, ox, ox2, oz,
        sc, sb, sy, sy2, sx, sx2, sz,
        uc, ub, ux, ux2, uz, uz2, uy,
        dc, db, dy, dy2, dx, dx2, dz,
        hx, h0, h2, hz,
        a_r, a_s, u_r, u_s, d_r, d_f, d_s, h_r, h_s,
    ) = scratch
    spot = Spot()
    y, c, z, x = spot.y, spot.c, spot.z, spot.x
    to_x, to_y, to_c = spot.at(x=1 - x), spot.at(y=1 - y), spot.at(c=1 - c)
    far = spot.at(y=1 - y, c=1 - c)
    quarter = y * 2 + c
    half, wide = GU.shape[0] // 2, GU.shape[1] // 8
    greet(spot, (far,))
    arrays = (
        (GQ, OQ, qc, qb, qy, qy2, qx, qx2, qz),
        (GO, OO, oc, ob, oy, oy2, ox, ox2, oz),
        (SM, OS, sc, sb, sy, sy2, sx, sx2, sz),
    )

    for i, (full, out, rc, bc, *rest) in enumerate(arrays):
        send(full.at[:, 1 - c], rc, a_s.at[i, 0], a_r.at[i, 0], to_c)
    send(
        GU.at[pl.ds(pl.multiple_of((1 - c) * half, half), half), :],
        uc, u_s.at[0], u_r.at[0], to_c,
    )
    send(GD.at[:, :, :, 1 - c], dc, d_s.at[0], d_r.at[0], to_c)
    send(HN.at[3], hx.at[0], h_s.at[0], h_r.at[0], to_x)
    send(HN.at[1], hx.at[1], h_s.at[1], h_r.at[1], to_x)

    for i, (full, out, rc, bc, ry, by, *rest) in enumerate(arrays):
        take(rc, a_r.at[i, 0])

        def step(n, full=full, rc=rc, bc=bc):
            yy, zz, xx = n // 8, (n // 2) % 4, n % 2
            bc[yy, zz, xx] = (f32(full[yy, c, zz, xx]) + f32(rc[yy, zz, xx])).astype(bc.dtype)

        add_pieces(16, step)
        send(bc.at[1 - y], ry, a_s.at[i, 1], a_r.at[i, 1], to_y)

    take(uc, u_r.at[0])

    def up_core(n):
        rows = pl.ds(pl.multiple_of(n * 16, 16), 16)
        mine = pl.ds(pl.multiple_of(c * half + n * 16, 16), 16)
        for s in range(8):
            cols = slice(s * wide, (s + 1) * wide)
            ub[s, rows, :] = (f32(GU[mine, cols]) + f32(uc[rows, cols])).astype(jnp.bfloat16)

    add_pieces(half // 16, up_core)
    for zz in range(4):
        send(ub.at[zz * 2 + (1 - x)], ux.at[zz], u_s.at[1], u_r.at[1], to_x)

    take(dc, d_r.at[0])

    def down_core(n):
        zz, xx, yy = n // 4, (n // 2) % 2, n % 2
        db[yy, zz, xx] = (f32(GD[zz, xx, yy, c]) + f32(dc[zz, xx, yy])).astype(jnp.bfloat16)

    add_pieces(16, down_core)
    send(db.at[1 - y], dy, d_s.at[1], d_r.at[1], to_y)

    take(hx.at[0], h_r.at[0])
    take(hx.at[1], h_r.at[1])

    def rows_x(n):
        rows = pl.ds(pl.multiple_of(n * 16, 16), 16)
        first, second = f32(hx[0, rows]), f32(hx[1, rows])
        h2[rows] = (f32(HN[2, rows]) + jnp.where(x == 1, first, second)).astype(jnp.bfloat16)
        h0[rows] = (f32(HN[0, rows]) + jnp.where(x == 1, second, 0.0)).astype(jnp.bfloat16)
        OH[rows] = jnp.where(x == 0, first, 0.0)

    add_pieces(HN.shape[1] // 16, rows_x)

    @pl.when(z >= 1)
    def _():
        send(h0, hz.at[0], h_s.at[2], h_r.at[2], spot.at(z=z - 1))

    for i, (full, out, rc, bc, ry, by, rx, *rest) in enumerate(arrays):
        take(ry, a_r.at[i, 1])

        def step(n, bc=bc, ry=ry, by=by):
            zz, xx = n // 2, n % 2
            by[xx, zz] = (f32(bc[y, zz, xx]) + f32(ry[zz, xx])).astype(by.dtype)

        add_pieces(8, step)
        send(by.at[1 - x], rx, a_s.at[i, 2], a_r.at[i, 2], to_x)

    take(ux, u_r.at[1])

    def up_x(n):
        zz = n // 24
        rows = pl.ds(pl.multiple_of((n % 24) * 16, 16), 16)
        ux2[zz, rows] = (f32(ub[zz * 2 + x, rows]) + f32(ux[zz, rows])).astype(jnp.bfloat16)

    add_pieces(96, up_x)
    for k in (1, 3, 2):
        send(ux2.at[spot.turn(k)], uz.at[3 - k], u_s.at[2], u_r.at[2], spot.at(z=spot.turn(k)))

    @pl.when(z <= 2)
    def _():
        take(hz.at[0], h_r.at[2])

        def rows_z(n):
            rows = pl.ds(pl.multiple_of(n * 16, 16), 16)
            h2[rows] = (f32(h2[rows]) + f32(hz[0, rows])).astype(jnp.bfloat16)

        add_pieces(HN.shape[1] // 16, rows_z)

    @pl.when(z >= 1)
    def _():
        send(h2, hz.at[1], h_s.at[3], h_r.at[3], spot.at(z=z - 1))

    take(dy, d_r.at[1])

    def down_y(n):
        zz, xx = n // 2, n % 2
        dy2[xx, zz] = (f32(db[y, zz, xx]) + f32(dy[zz, xx])).astype(jnp.bfloat16)

    add_pieces(8, down_y)
    send(dy2.at[1 - x], dx, d_s.at[2], d_r.at[2], to_x)

    for i, (full, out, rc, bc, ry, by, rx, bx, rz) in enumerate(arrays):
        take(rx, a_r.at[i, 2])

        def step(n, by=by, rx=rx, bx=bx):
            bx[n] = (f32(by[x, n]) + f32(rx[n])).astype(bx.dtype)

        add_pieces(4, step)
        for k in (1, 3, 2):
            send(
                bx.at[spot.turn(k)], rz.at[3 - k], a_s.at[i, 3], a_r.at[i, 3],
                spot.at(z=spot.turn(k)),
            )

    take(dx, d_r.at[2])

    def down_x(n):
        dx2[n] = (f32(dy2[x, n]) + f32(dx[n])).astype(jnp.bfloat16)

    add_pieces(4, down_x)
    for k in (1, 3, 2):
        send(dx2.at[spot.turn(k)], dz.at[3 - k], d_s.at[3], d_r.at[3], spot.at(z=spot.turn(k)))

    take(uz, u_r.at[2])

    def up_z(n):
        rows = pl.ds(pl.multiple_of(n * 16, 16), 16)
        total = f32(ux2[z, rows]) + f32(uz[0, rows]) + f32(uz[1, rows]) + f32(uz[2, rows])
        uz2[rows] = total.astype(jnp.bfloat16)

    add_pieces(24, up_z)
    send(uz2, uy, u_s.at[3], u_r.at[3], to_y)

    for i, (full, out, rc, bc, ry, by, rx, bx, rz) in enumerate(arrays):
        take(rz, a_r.at[i, 3])
        out[...] = f32(bx[z]) + f32(rz[0]) + f32(rz[1]) + f32(rz[2])

    take(dz, d_r.at[3])
    done = f32(dx2[z]) + f32(dz[0]) + f32(dz[1]) + f32(dz[2])
    OD[quarter] = done.astype(jnp.bfloat16)
    for n, device in enumerate((to_y, to_c, far)):
        send(OD.at[quarter], OD.at[quarter], d_s.at[4], d_f.at[n], device)

    take(uy, u_r.at[3])

    def up_y(n):
        rows = pl.ds(pl.multiple_of(n * 16, 16), 16)
        OU[c, rows] = (f32(uz2[rows]) + f32(uy[rows])).astype(jnp.bfloat16)

    add_pieces(24, up_y)
    send(OU.at[c], OU.at[c], u_s.at[4], u_r.at[4], to_c)

    @pl.when(z <= 2)
    def _():
        take(hz.at[1], h_r.at[3])

        def rows_own(n):
            rows = pl.ds(pl.multiple_of(n * 16, 16), 16)
            OH[rows] = OH[rows] + f32(hz[1, rows])

        add_pieces(HN.shape[1] // 16, rows_own)

    take(OD.at[0], d_f.at[0])
    take(OD.at[0], d_f.at[1])
    take(OD.at[0], d_f.at[2])
    take(OU.at[0], u_r.at[4])

    for i, (full, out, rc, bc, ry, by, rx, bx, rz) in enumerate(arrays):
        take(rc, a_s.at[i, 0])
        take(ry, a_s.at[i, 1])
        take(rx, a_s.at[i, 2])
        take(rz, a_s.at[i, 3])
    for n, ref in enumerate((uc, ux, uz, uy, uz2)):
        take(ref, u_s.at[n])
    for n, ref in enumerate((dc, dy, dx, dz, dz)):
        take(ref, d_s.at[n])
    take(h0, h_s.at[0])
    take(h0, h_s.at[1])

    @pl.when(z >= 1)
    def _():
        take(h0, h_s.at[2])
        take(h0, h_s.at[3])


def reduce_all(qkv, out, small, up, down, halo):
    bf = jnp.bfloat16
    width = out.shape[1]
    deep = width // 32
    rows = halo.shape[1]
    qkv = qkv.reshape(2, 2, 4, 2, deep, qkv.shape[1])
    out = out.reshape(2, 2, 4, 2, deep, width)
    small = small.reshape(2, 2, 4, 2, deep, small.shape[1])
    ff = up.shape[1]
    wide, piece = ff // 8, ff // 32
    down = down.reshape(4, 2, 2, 2, piece, width)
    scratch = []
    for array in (qkv, out, small):
        tail, kind = array.shape[4:], array.dtype
        for lead in ((2, 4, 2), (2, 4, 2), (4, 2), (2, 4), (4,), (4,), (3,)):
            scratch.append(pltpu.VMEM(lead + tail, kind))
    half = width // 2
    for shape in (
        (half, ff), (8, half, wide), (4, half, wide), (4, half, wide), (3, half, wide),
        (half, wide), (half, wide),
    ):
        scratch.append(pltpu.VMEM(shape, bf))
    for lead in ((4, 2, 2), (2, 4, 2), (4, 2), (2, 4), (4,), (4,), (3,)):
        scratch.append(pltpu.VMEM(lead + (piece, width), bf))
    for lead in ((2,), (), (), (2,)):
        scratch.append(pltpu.VMEM(lead + (rows, width), bf))
    dma = pltpu.SemaphoreType.DMA
    for shape in ((3, 4), (3, 4), (5,), (5,), (4,), (3,), (5,), (4,), (4,)):
        scratch.append(dma(shape))
    return pl.pallas_call(
        reduce_kernel,
        out_shape=(
            jax.ShapeDtypeStruct((deep, qkv.shape[-1]), jnp.float32),
            jax.ShapeDtypeStruct((deep, width), jnp.float32),
            jax.ShapeDtypeStruct((deep, small.shape[-1]), jnp.float32),
            jax.ShapeDtypeStruct((2, half, wide), bf),
            jax.ShapeDtypeStruct((4, piece, width), bf),
            jax.ShapeDtypeStruct((rows, width), jnp.float32),
        ),
        in_specs=[pl.BlockSpec(memory_space=pltpu.VMEM)] * 6,
        out_specs=[pl.BlockSpec(memory_space=pltpu.VMEM)] * 6,
        scratch_shapes=scratch,
        compiler_params=pltpu.CompilerParams(
            collective_id=1, has_side_effects=True, vmem_limit_bytes=VMEM_LIMIT
        ),
        name="reduce_gradients",
    )(qkv, out, small, up, down, halo)


def attend_kernel(q_ref, k_ref, v_ref, bias_ref, o_ref, inv_ref, p_ref):
    queries, keys = q_ref[...], k_ref[...]
    lane = lax.broadcasted_iota(jnp.int32, queries.shape, 1)
    values_t = v_ref[...].T
    parts = []
    for h in range(2):
        own = (lane // HEAD_DIM) == h
        one = jnp.where(own, queries, jnp.zeros_like(queries))
        scores = contract_last(keys, one) + bias_ref[...]
        shifted = jnp.exp(scores - jnp.max(scores, axis=0, keepdims=True))
        inverse = 1.0 / jnp.sum(shifted, axis=0, keepdims=True)
        probs = shifted.astype(jnp.bfloat16)
        p_ref[h] = probs
        inv_ref[0, h : h + 1, :] = inverse
        rows = values_t[h * HEAD_DIM : (h + 1) * HEAD_DIM]
        parts.append(jnp.dot(rows, probs, preferred_element_type=jnp.float32) * inverse)
    o_ref[...] = jnp.concatenate(parts, axis=0).T


def attend(queries, keys, values, bias):
    rows, width = queries.shape
    span = keys.shape[0]
    pairs = width // (2 * HEAD_DIM)
    across = 2 * HEAD_DIM
    return pl.pallas_call(
        attend_kernel,
        grid=(pairs,),
        out_shape=(
            jax.ShapeDtypeStruct((rows, width), jnp.float32),
            jax.ShapeDtypeStruct((pairs, 8, rows), jnp.float32),
            jax.ShapeDtypeStruct((2 * pairs, span, rows), jnp.bfloat16),
        ),
        in_specs=[
            pl.BlockSpec((rows, across), lambda i: (0, i)),
            pl.BlockSpec((span, across), lambda i: (0, i)),
            pl.BlockSpec((span, across), lambda i: (0, i)),
            pl.BlockSpec((span, rows), lambda i: (0, 0)),
        ],
        out_specs=[
            pl.BlockSpec((rows, across), lambda i: (0, i)),
            pl.BlockSpec((1, 8, rows), lambda i: (i, 0, 0)),
            pl.BlockSpec((2, span, rows), lambda i: (i, 0, 0)),
        ],
        compiler_params=pltpu.CompilerParams(vmem_limit_bytes=VMEM_LIMIT),
        name="attend",
    )(queries, keys, values, bias)


def attend_back_kernel(q_ref, k_ref, v_ref, g_ref, o_ref, inv_ref, p_ref, dq_ref, dk_ref, dv_ref):
    queries, values = q_ref[...], v_ref[...]
    grad_t = f32(g_ref[...]).T
    att_t = o_ref[...].T
    keys_t = k_ref[...].T
    span = values.shape[0]
    scaled_t = jnp.concatenate(
        [
            grad_t[h * HEAD_DIM : (h + 1) * HEAD_DIM] * inv_ref[0, h : h + 1, :]
            for h in range(2)
        ],
        axis=0,
    )
    scaled = scaled_t.T.astype(jnp.bfloat16)
    product = scaled_t * att_t
    low_t = scaled_t.astype(jnp.bfloat16)
    row = lax.broadcasted_iota(jnp.int32, low_t.shape, 0)
    parts, key_parts, value_parts = [], [], []
    for h in range(2):
        delta = jnp.sum(product[h * HEAD_DIM : (h + 1) * HEAD_DIM], axis=0, keepdims=True)
        one = jnp.where((row // HEAD_DIM) == h, low_t, jnp.zeros_like(low_t))
        prob_grad = jnp.dot(values, one, preferred_element_type=jnp.float32)
        probs = p_ref[h]
        score_grad = (f32(probs) * (prob_grad - delta)).astype(jnp.bfloat16)
        key_parts.append(jnp.dot(score_grad, queries, preferred_element_type=jnp.float32))
        value_parts.append(jnp.dot(probs, scaled, preferred_element_type=jnp.float32))
        parts.append(
            jnp.dot(
                keys_t[h * HEAD_DIM : (h + 1) * HEAD_DIM],
                score_grad,
                preferred_element_type=jnp.float32,
            )
        )
    dq_ref[...] = jnp.concatenate(parts, axis=0).T * HEAD_DIM ** (-0.5)
    first = lax.broadcasted_iota(jnp.int32, (span, 2 * HEAD_DIM), 1) < HEAD_DIM
    dk_ref[...] = jnp.where(first, key_parts[0], key_parts[1])
    dv_ref[...] = jnp.where(first, value_parts[0], value_parts[1])


def attend_back(queries, keys, values, grad, attended, inverse, probs):
    rows, width = queries.shape
    span = keys.shape[0]
    pairs = width // (2 * HEAD_DIM)
    across = 2 * HEAD_DIM
    narrow = pl.BlockSpec((rows, across), lambda i: (0, i))
    long = pl.BlockSpec((span, across), lambda i: (0, i))
    return pl.pallas_call(
        attend_back_kernel,
        grid=(pairs,),
        out_shape=(
            jax.ShapeDtypeStruct((rows, width), jnp.float32),
            jax.ShapeDtypeStruct((span, width), jnp.float32),
            jax.ShapeDtypeStruct((span, width), jnp.float32),
        ),
        in_specs=[
            narrow,
            long,
            long,
            narrow,
            narrow,
            pl.BlockSpec((1, 8, rows), lambda i: (i, 0, 0)),
            pl.BlockSpec((2, span, rows), lambda i: (i, 0, 0)),
        ],
        out_specs=[narrow, long, long],
        compiler_params=pltpu.CompilerParams(vmem_limit_bytes=VMEM_LIMIT),
        name="attend_back",
    )(queries, keys, values, grad, attended, inverse, probs)


def shifted_down(array, lag):
    if lag == 0:
        return array
    return jnp.pad(array[:-lag], ((lag, 0), (0, 0)))


def shifted_up(array, lag):
    if lag == 0:
        return array
    return jnp.pad(array[lag:], ((0, lag), (0, 0)))


def on_device_blocks(
    block_in, segment_ids, w_qkv, w_out, conv_taps, norm_gain, norm_bias, w_up, w_down, out_grad
):
    rows, width = block_in.shape
    seq_len = segment_ids.shape[0]
    reach = seq_len // rows
    behind = reach // 2
    span = (behind + 1) * rows
    deep = w_qkv.shape[0]
    bf = jnp.bfloat16
    model_index = lax.axis_index("mp")
    start = model_index * rows
    edge = 16

    small = jnp.concatenate(
        [f32(norm_gain), f32(norm_bias), f32(conv_taps).reshape(deep, 9)], axis=1
    )
    small = jnp.pad(small, ((0, 0), (0, 128 - small.shape[1])))
    WQ, WO, PR, WU, WD, XW = gather_all(w_qkv, w_out, small, w_up, w_down, block_in)
    full_qkv = WQ.reshape(width, 3 * width)
    full_out = WO.reshape(width, width)
    params = PR.reshape(width, 128).T
    gains, biases = params[0:2], params[2:4]
    taps = params[4:13].reshape(3, 3, width).transpose(1, 0, 2).reshape(3, 3 * width)
    full_down = WD.reshape(w_down.shape[0] * 8, width)

    padded = jnp.concatenate([jnp.full((behind * rows,), -1, jnp.int32), segment_ids])
    segs = lax.dynamic_slice_in_dim(padded, start, span)
    place = jnp.arange(span, dtype=jnp.int32)
    allowed = (segs[:, None] == segs[None, span - rows :]) & (
        place[:, None] <= place[None, span - rows :]
    )
    bias = jnp.where(allowed, 0.0, -1e30)
    keeps = [
        jnp.concatenate([jnp.zeros((lag,), bool), segs[lag:] == segs[: span - lag]])[:, None]
        for lag in range(3)
    ]

    blocks = jnp.arange(behind + 1) + model_index >= behind
    window = jnp.where(blocks[:, None, None], XW, jnp.zeros_like(XW)).reshape(span, width)
    window = f32(window)
    normed1_full, normal1, inverse1 = layer_norm(window, gains[0:1], biases[0:1])
    normed1 = normed1_full.astype(bf)
    late = span - rows - edge

    def convolve(pre, keep, own_taps):
        total = jnp.zeros(pre.shape, jnp.float32)
        for lag in range(3):
            total = total + jnp.where(keep[lag], shifted_down(pre, lag), 0.0) * own_taps[lag]
        return total

    keeps_q = [k[late:] for k in keeps]
    pre_q = jnp.dot(normed1[late:], full_qkv[:, :width], preferred_element_type=jnp.float32)
    pre_kv = jnp.dot(normed1, full_qkv[:, width:], preferred_element_type=jnp.float32)
    mixed_q = convolve(pre_q, keeps_q, taps[:, :width])[edge:].astype(bf)
    mixed_kv = convolve(pre_kv, keeps, taps[:, width:]).astype(bf)
    keys, values = mixed_kv[:, :width], mixed_kv[:, width:]
    queries = mixed_q * jnp.asarray(HEAD_DIM ** (-0.5), bf)
    attended_f32, inverse_sum, probs = attend(queries, keys, values, bias)
    attended = attended_f32.astype(bf)
    residual = f32(block_in) + jnp.dot(attended, full_out, preferred_element_type=jnp.float32)
    normed2_full, normal2, inverse2 = layer_norm(residual, gains[1:2], biases[1:2])
    normed2 = normed2_full.astype(bf)
    upper = jnp.maximum(jnp.dot(normed2, WU, preferred_element_type=jnp.float32), 0.0)
    hidden = jnp.square(upper).astype(bf)
    ff_out = jnp.dot(hidden, full_down, preferred_element_type=jnp.float32)
    block_out = (residual + ff_out).astype(bf)

    hidden_grad = contract_last(out_grad, full_down)
    upper_grad = (2.0 * upper * hidden_grad).astype(bf)
    down_local = contract_first(hidden, out_grad).astype(bf)
    up_local = contract_first(normed2, upper_grad).astype(bf)
    normed2_grad = contract_last(upper_grad, WU)
    back2, gain2_grad, bias2_grad = norm_back(normed2_grad, normal2, inverse2, gains[1:2])
    residual_grad = f32(out_grad) + back2
    mixed_grad = residual_grad.astype(bf)
    proj_local = contract_first(attended, mixed_grad).astype(bf)
    attended_grad = contract_last(mixed_grad, full_out).astype(bf)

    query_grad, key_grad, value_grad = attend_back(
        queries, keys, values, attended_grad, attended_f32, inverse_sum, probs
    )
    query_grad = jnp.pad(query_grad, ((edge, 0), (0, 0)))
    pair_grad = jnp.concatenate([key_grad, value_grad], axis=1)

    def convolve_back(grad, keep, own_taps):
        total = jnp.zeros(grad.shape, jnp.float32)
        for lag in range(3):
            total = total + shifted_up(jnp.where(keep[lag], grad, 0.0), lag) * own_taps[lag]
        return total.astype(bf)

    def taps_sum(pre, grad, keep):
        return jnp.stack(
            [
                jnp.sum(jnp.where(keep[lag], shifted_down(pre, lag) * grad, 0.0), axis=0)
                for lag in range(3)
            ]
        )

    pre_grad_q = convolve_back(query_grad, keeps_q, taps[:, :width])
    pre_grad_kv = convolve_back(pair_grad, keeps, taps[:, width:])
    conv_local = jnp.concatenate(
        [taps_sum(pre_q, query_grad, keeps_q), taps_sum(pre_kv, pair_grad, keeps)], axis=1
    )
    conv_local = conv_local.reshape(3, 3, width).transpose(2, 1, 0).reshape(width, 9)
    qkv_local = jnp.concatenate(
        [contract_first(normed1[late:], pre_grad_q), contract_first(normed1, pre_grad_kv)], axis=1
    ).astype(bf)
    grad_kv = contract_last(pre_grad_kv, full_qkv[:, width:])
    grad_q = contract_last(pre_grad_q, full_qkv[:, :width])
    normed1_grad = grad_kv + jnp.pad(grad_q, ((late, 0), (0, 0)))
    gain1_grad = jnp.sum(normed1_grad * normal1, axis=0)
    bias1_grad = jnp.sum(normed1_grad, axis=0)
    small_local = jnp.concatenate(
        [
            jnp.stack([gain1_grad, gain2_grad, bias1_grad, bias2_grad], axis=1),
            conv_local,
            jnp.zeros((width, 128 - 13), jnp.float32),
        ],
        axis=1,
    )
    halo = normed1_grad[: behind * rows].astype(bf).reshape(behind, rows, width)
    qkv_grad, proj_grad, small_grad, up_grad, down_grad, halo_grad = reduce_all(
        qkv_local, proj_local, small_local, up_local, down_local, halo
    )
    own_grad = normed1_grad[behind * rows :] + halo_grad
    back1, _, _ = norm_back(
        own_grad, normal1[behind * rows :], inverse1[behind * rows :], gains[0:1]
    )
    return (
        block_out,
        residual_grad + back1,
        qkv_grad,
        proj_grad,
        small_grad[:, 4:13].reshape(deep, 3, 3),
        small_grad[:, 0:2],
        small_grad[:, 2:4],
        f32(up_grad).reshape(width, w_up.shape[1]),
        f32(down_grad).reshape(w_down.shape[0], width),
    )


def solution(mesh):
    in_specs = (
        P(("dp", "mp"), None),
        P("dp"),
        P(("dp", "mp"), None),
        P(("dp", "mp"), None),
        P(("dp", "mp"), None, None),
        P(("dp", "mp"), None),
        P(("dp", "mp"), None),
        P(None, "mp"),
        P("mp", None),
        P(("dp", "mp"), None),
    )
    out_specs = (
        P(("dp", "mp"), None),
        P(("dp", "mp"), None),
        P(("dp", "mp"), None),
        P(("dp", "mp"), None),
        P(("dp", "mp"), None, None),
        P(("dp", "mp"), None),
        P(("dp", "mp"), None),
        P(None, "mp"),
        P("mp", None),
    )
    known = dict(mesh.shape) == {"dp": 4, "mp": 8}
    on_device = on_device_blocks if known else on_device_rings
    return jax.shard_map(
        on_device, mesh=mesh, in_specs=in_specs, out_specs=out_specs, check_vma=False
    )
```
